512 devices in a mesh: dp: 64 (over x, z_hi, y, core), bfly: 8 (over z_lo).
Axes of the slice: x: 4, y: 4, z: 16 (z_hi: 2, z_lo: 8; z = z_hi * 8 + z_lo), core: 2. Of those that a mesh axis runs over, the one named last changes fastest.
Arguments:
- features: bfloat16 [8192, 8192], P('dp', 'bfly'), may hold values from -6 to 6
- weight: bfloat16 [4, 256, 14336], P(None, 'dp', 'bfly'), may hold values from -0.1875 to 0.1875
- block_table: int32 [4, 56], P(None, 'bfly'), may hold values from 0 to 3
- upstream: bfloat16 [8192, 14336], P('dp', 'bfly'), may hold values from -6 to 6
Outputs:
- activation: bfloat16 [8192, 14336], P('dp', 'bfly')
- input_grad: bfloat16 [8192, 8192], P('dp', 'bfly')
- weight_grad: float32 [4, 256, 14336], P(None, 'dp', 'bfly')
The draws below stay inside these ranges and needn't reach their ends.
Inputs may be any that keep to these rules, and one draw needn't show every extreme that they name: block_table[s, k] names a feature block within the partner group of hidden block k at section s.
All inputs are finite; a program needn't handle non-finite values.
Results may differ from the reference program's by a relative error of at most 0.0058.
Values may be sent and summed in bfloat16 or wider, within the bound.
No kernel may reach another device: no remote copies, remote signals or barrier semaphores. Data moves between devices by JAX's collectives and lax.ppermute only.
A program may use at most 64 MiB of HBM per device.

```python
import jax
import jax.numpy as jnp
from jax import lax

D = 8192
FF = 14336
BLK = 256
SECTIONS = 4
TOKENS = 8192
FBLK = 4
HBLK = 56
N_BFLY = 8


def with_ends(array, key, low, top_value):
    dims = array.shape
    index_at = [jax.random.randint(jax.random.fold_in(key, axis), (), 0, dims[axis]) for axis in range(len(dims))]
    array = array.at[tuple(index_at)].set(low)
    longest = dims.index(max(dims))
    index_at[longest] = (index_at[longest] + 1) % dims[longest]
    return array.at[tuple(index_at)].set(top_value)


def level_of(key, dims, split, low, largest):
    level, own = 1.0, jax.random.fold_in(key, 6)
    for axis_at, shards_of in split:
        steps = jnp.exp(jax.random.uniform(jax.random.fold_in(own, axis_at), (shards_of,), jnp.float32, low / len(split), largest / len(split)))
        level = level * jnp.repeat(steps, dims[axis_at] // shards_of).reshape([-1 if axis == axis_at else 1 for axis in range(len(dims))])
    return level


def bell_draw(key, dims, scale, most, pieces=(), kind=jnp.bfloat16):
    result = jax.random.normal(key, dims, jnp.float32) * scale
    if len(pieces) > 0:
        result = level_of(key, dims, pieces, -0.22, 0.18) * result
    return jnp.clip(result, min=-most, max=most).astype(kind)


def setup_inputs(seed: int = 0) -> dict:
    streams_of = jax.random.split(jax.random.key(seed), 5)
    return {
        "features": bell_draw(streams_of[0], (TOKENS, D), 1.0, 6.0, ((0, 64), (1, 8))),
        "weight": bell_draw(streams_of[1], (SECTIONS, BLK, FF), (SECTIONS * BLK) ** -0.5, 0.1875, ((1, 64), (2, 8))),
        "block_table": with_ends(jax.random.randint(streams_of[2], (SECTIONS, HBLK), 0, FBLK), jax.random.fold_in(streams_of[2], 1), 0, FBLK - 1).astype(jnp.int32),
        "upstream": bell_draw(streams_of[3], (TOKENS, FF), 1.0, 6.0, ((0, 64), (1, 8))),
    }


half_root = 0.7071067811865476
inv_root_tau = 0.3989422804014327


def gelu_pair(pre_act):
    normal_cdf = 0.5 * (1.0 + lax.erf(pre_act * half_root))
    density = jnp.exp(-0.5 * pre_act * pre_act) * inv_root_tau
    return pre_act * normal_cdf, normal_cdf + pre_act * density


def reference(features, weight, block_table, upstream):
    tokens = features.shape[0]
    feat_blocks = D // (BLK * N_BFLY)
    hidden_group = FF // (BLK * N_BFLY)
    bit_count = N_BFLY.bit_length() - 1
    own_slabs = features.reshape(tokens, N_BFLY, feat_blocks, BLK)
    weights = weight.reshape(SECTIONS, BLK, N_BFLY, hidden_group, BLK).astype(jnp.float32)
    table = block_table.reshape(SECTIONS, N_BFLY, hidden_group)
    cotangent = upstream.reshape(tokens, N_BFLY, hidden_group, BLK).astype(jnp.float32)
    columns = jnp.arange(feat_blocks, dtype=jnp.int32)
    grad_scale = float(tokens) ** -0.5
    activations = []
    gradients = []
    input_grad = jnp.zeros((tokens, N_BFLY, feat_blocks, BLK), jnp.float32)
    for own_group in range(N_BFLY):
        partners = [own_group] + [own_group ^ (1 << ((section_index - 1) % bit_count)) for section_index in range(1, SECTIONS)]
        gathered = jnp.stack(
            [jnp.take(own_slabs[:, partners[section_index]], table[section_index, own_group], axis=1) for section_index in range(SECTIONS)],
            axis=2).astype(jnp.float32)
        group_weight = weights[:, :, own_group]
        pre_act = jnp.einsum("tjsc,scjd->tjd", gathered, group_weight)
        activated, slope_term = gelu_pair(pre_act)
        activations.append(activated.astype(jnp.bfloat16))
        grad_low = lax.optimization_barrier((cotangent[:, own_group] * slope_term).astype(jnp.bfloat16))
        grad_pre = grad_low.astype(jnp.float32)
        gradients.append(jnp.einsum("tjsc,tjd->scjd", gathered, grad_pre) * grad_scale)
        back_terms = jnp.einsum("tjd,scjd->tjsc", grad_pre, group_weight)
        shares = {}
        for section_index in range(SECTIONS):
            onehot = (table[section_index, own_group][:, None] == columns[None, :]).astype(jnp.float32)
            placed = jnp.einsum("jb,tjc->tbc", onehot, back_terms[:, :, section_index],
                                precision=lax.Precision.HIGHEST)
            target = partners[section_index]
            shares[target] = placed if target not in shares else shares[target] + placed
        for target in shares:
            rounded = lax.optimization_barrier(shares[target].astype(jnp.bfloat16))
            input_grad = input_grad.at[:, target].add(rounded.astype(jnp.float32))
    activation = jnp.stack(activations, axis=1).reshape(tokens, FF)
    weight_grad = jnp.stack(gradients, axis=2).reshape(SECTIONS, BLK, FF)
    return activation, input_grad.reshape(tokens, D).astype(jnp.bfloat16), weight_grad
```

```python
import jax
import jax.numpy as jnp
import numpy as np
from jax import lax
from jax.experimental import pallas as pl
from jax.experimental.pallas import tpu as pltpu
from jax.sharding import Mesh
from jax.sharding import PartitionSpec as P

half_root = 0.7071067811865476
inv_root_tau = 0.3989422804014327
XS, ZS, YS, CS = 4, 2, 4, 2
DP = ("x", "zh", "y", "core")
PLANE = ("x", "y")
VMEM_LIMIT = 40 * 1024 * 1024


def swapped(block, stride):
    count = lax.axis_size("bfly")
    return lax.ppermute(block, "bfly", [(low, low ^ (1 << stride)) for low in range(count)])


def flipped(block, axis):
    return lax.ppermute(block, axis, [(0, 1), (1, 0)])


def vmem():
    return pl.BlockSpec(memory_space=pltpu.VMEM)


def smem():
    return pl.BlockSpec(memory_space=pltpu.SMEM)


def params(limit=VMEM_LIMIT):
    return pltpu.CompilerParams(vmem_limit_bytes=limit)


def columns_of(block):
    return pl.ds(pl.multiple_of(block * 256, 256), 256)


def forward_kernel(tab, f0, f1, f2, f3, w00, w01, w10, w11, up, order, act, grad, wn):
    feats = (f0, f1, f2, f3)
    sections, hidden_blocks = tab.shape
    for x in range(XS):
        rows = jnp.concatenate([w00[x], w01[x], w10[x], w11[x]], axis=0)
        natural = jnp.dot(order[...], rows, preferred_element_type=jnp.float32).astype(jnp.bfloat16)
        for s in range(sections):
            wn[s, x * 64 : (x + 1) * 64, :] = natural[s * 64 : (s + 1) * 64]
    for j in range(hidden_blocks):
        cols = slice(j * 256, (j + 1) * 256)
        pre = None
        for s in range(sections):
            term = jnp.dot(feats[s][:, columns_of(tab[s, j])], wn[s, :, cols], preferred_element_type=jnp.float32)
            pre = term if pre is None else pre + term
        cdf = 0.5 * (1.0 + lax.erf(pre * half_root))
        density = jnp.exp(-0.5 * pre * pre) * inv_root_tau
        act[:, cols] = (pre * cdf).astype(jnp.bfloat16)
        grad[:, cols] = (up[:, cols].astype(jnp.float32) * (cdf + pre * density)).astype(jnp.bfloat16)


def weight_kernel(tab, f0, f1, f2, f3, grad, order, keep, send, ft, terms):
    feats = (f0, f1, f2, f3)
    sections, hidden_blocks = tab.shape
    for s in range(sections):
        for b in range(4):
            ft[s, b] = feats[s][:, b * 256 : (b + 1) * 256].T
    for j in range(hidden_blocks):
        cols = slice(j * 256, (j + 1) * 256)
        for s in range(sections):
            term = jnp.dot(ft[s, tab[s, j]], grad[:, cols], preferred_element_type=jnp.float32).astype(jnp.bfloat16)
            for x in range(XS):
                terms[x, s * 64 : (s + 1) * 64, cols] = term[x * 64 : (x + 1) * 64]
    for x in range(XS):
        rows = jnp.dot(order[...], terms[x], preferred_element_type=jnp.float32).astype(jnp.bfloat16)
        keep[x] = rows[:128]
        send[x] = rows[128:]


def share_kernel(tab, grad, wn, s0, s1, s2, s3, total):
    shares = (s0, s1, s2, s3)
    sections, hidden_blocks = tab.shape
    for s in range(sections):
        total[...] = jnp.zeros_like(total)
        for j in range(hidden_blocks):
            cols = slice(j * 256, (j + 1) * 256)
            place = columns_of(tab[s, j])
            total[:, place] += lax.dot_general(
                grad[:, cols], wn[s, :, cols], (((1,), (1,)), ((), ())), preferred_element_type=jnp.float32
            )
        shares[s][...] = total[...].astype(jnp.bfloat16)


def orders():
    core, half = lax.axis_index("core"), lax.axis_index("zh")
    row = lax.broadcasted_iota(jnp.int32, (256, 256), 0)
    col = lax.broadcasted_iota(jnp.int32, (256, 256), 1)

    def natural(s, z, y, c, r):
        return s * 64 + z * 32 + y * 8 + c * 4 + r

    stored = natural(
        (col // 4) % 4, ((col // 64) % 2) ^ half, (col // 16) % 4, (col // 128) ^ core, col % 4
    )
    gather = (row == stored).astype(jnp.bfloat16)
    sent = natural((row // 4) % 4, (row // 16) % 2, (row // 32) % 4, (row // 128) ^ core, row % 4)
    scatter = (col == sent).astype(jnp.bfloat16)
    return gather, scatter


def spread(shard):
    everyone = jnp.broadcast_to(shard[None], (XS * YS, *shard.shape))
    got = lax.all_to_all(everyone, PLANE, split_axis=0, concat_axis=0, tiled=True)
    return got.reshape(XS, YS * shard.shape[0], shard.shape[1])


def body(features, weight, block_table, upstream):
    tok_rows = features.shape[0]
    sections, shard_rows, width = weight.shape
    bf16 = jnp.bfloat16
    gather, scatter = orders()

    shard = weight.reshape(sections * shard_rows, width)
    w00 = spread(shard)
    far = flipped(shard, "zh")
    feats = [features] + [swapped(features, bit) for bit in range(3)]
    w10 = flipped(w00, "core")
    w01 = spread(far)
    w11 = flipped(w01, "core")

    act, grad, wn = pl.pallas_call(
        forward_kernel,
        out_shape=(
            jax.ShapeDtypeStruct((tok_rows, width), bf16),
            jax.ShapeDtypeStruct((tok_rows, width), bf16),
            jax.ShapeDtypeStruct((sections, 256, width), bf16),
        ),
        in_specs=[smem()] + [vmem()] * 10,
        out_specs=(vmem(), vmem(), vmem()),
        compiler_params=params(),
        name="forward",
    )(block_table, *feats, w00, w01, w10, w11, upstream, gather)

    half_shape = jax.ShapeDtypeStruct((XS, 128, width), bf16)
    keep, send = pl.pallas_call(
        weight_kernel,
        out_shape=(half_shape, half_shape),
        in_specs=[smem()] + [vmem()] * 6,
        out_specs=(vmem(), vmem()),
        scratch_shapes=[
            pltpu.VMEM((sections, 4, 256, tok_rows), bf16),
            pltpu.VMEM((XS, 256, width), bf16),
        ],
        compiler_params=params(),
        name="weight_grad",
    )(block_table, *feats, grad, scatter)
    got = flipped(send, "core")

    share = jax.ShapeDtypeStruct((tok_rows, features.shape[1]), bf16)
    shares = pl.pallas_call(
        share_kernel,
        out_shape=(share,) * 4,
        in_specs=[smem()] + [vmem()] * 2,
        out_specs=(vmem(),) * 4,
        scratch_shapes=[pltpu.VMEM((tok_rows, features.shape[1]), jnp.float32)],
        compiler_params=params(),
        name="shares",
    )(block_table, grad, wn)

    both = (keep.astype(jnp.float32) + got.astype(jnp.float32)).astype(bf16)
    both = both.reshape(XS * YS, 32, width)
    spread_rows = lax.all_to_all(both, PLANE, split_axis=0, concat_axis=0, tiled=True)
    arrived = [swapped(shares[bit + 1], bit) for bit in range(3)]
    summed = jnp.sum(spread_rows.astype(jnp.float32), axis=0)
    half = lax.axis_index("zh")
    mine = lax.dynamic_slice_in_dim(summed, half * 16, 16, 0)
    other = lax.dynamic_slice_in_dim(summed, (1 - half) * 16, 16, 0).astype(bf16)
    other = flipped(other, "zh")
    scale = float(tok_rows * XS * ZS * YS * CS) ** -0.5
    weight_grad = ((mine + other.astype(jnp.float32)) * scale).reshape(sections, shard_rows, width)

    input_grad = shares[0].astype(jnp.float32)
    for part in arrived:
        input_grad = input_grad + part.astype(jnp.float32)
    return act, input_grad.astype(bf16), weight_grad


def solution(mesh):
    fine = Mesh(mesh.devices.reshape(XS, ZS, YS, CS, mesh.shape["bfly"]), (*DP, "bfly"))
    return jax.shard_map(
        body,
        mesh=fine,
        in_specs=(P(DP, "bfly"), P(None, DP, "bfly"), P(None, "bfly"), P(DP, "bfly")),
        out_specs=(P(DP, "bfly"), P(DP, "bfly"), P(None, DP, "bfly")),
        check_vma=False,
    )
```

```python
import jax
import jax.numpy as jnp
from jax import lax
from jax.experimental import pallas as pl
from jax.experimental.pallas import tpu as pltpu
from jax.sharding import Mesh
from jax.sharding import PartitionSpec as P


half_root = 0.7071067811865476
inv_root_tau = 0.3989422804014327
XS, ZS, YS, CS = 4, 2, 4, 2
DP = ("x", "zh", "y", "core")
PLANE = ("x", "y")
VMEM_LIMIT = 20 * 1024 * 1024


def swapped(block, stride):
    count = lax.axis_size("bfly")
    return lax.ppermute(block, "bfly", [(low, low ^ (1 << stride)) for low in range(count)])


def flipped(block, axis):
    return lax.ppermute(block, axis, [(0, 1), (1, 0)])


def vmem():
    return pl.BlockSpec(memory_space=pltpu.VMEM)


def smem():
    return pl.BlockSpec(memory_space=pltpu.SMEM)


def params(limit=VMEM_LIMIT):
    return pltpu.CompilerParams(vmem_limit_bytes=limit)


def columns_of(block):
    return pl.ds(pl.multiple_of(block * 256, 256), 256)


def forward_kernel(tab, f0, f1, f2, f3, w00, w01, w10, w11, up, order, act, grad, wn):
    feats = (f0, f1, f2, f3)
    sections, hidden_blocks = tab.shape
    for x in range(XS):
        rows = jnp.concatenate([w00[x], w01[x], w10[x], w11[x]], axis=0)
        natural = jnp.dot(order[...], rows, preferred_element_type=jnp.float32).astype(jnp.bfloat16)
        for s in range(sections):
            wn[s, x * 64 : (x + 1) * 64, :] = natural[s * 64 : (s + 1) * 64]
    for j in range(hidden_blocks):
        cols = slice(j * 256, (j + 1) * 256)
        pre = None
        for s in range(sections):
            term = jnp.dot(feats[s][:, columns_of(tab[s, j])], wn[s, :, cols], preferred_element_type=jnp.float32)
            pre = term if pre is None else pre + term
        cdf = 0.5 * (1.0 + lax.erf(pre * half_root))
        density = jnp.exp(-0.5 * pre * pre) * inv_root_tau
        act[:, cols] = (pre * cdf).astype(jnp.bfloat16)
        grad[:, cols] = (up[:, cols].astype(jnp.float32) * (cdf + pre * density)).astype(jnp.bfloat16)


def weight_kernel(tab, f0, f1, f2, f3, grad, order, keep, send, ft, terms):
    feats = (f0, f1, f2, f3)
    sections, hidden_blocks = tab.shape
    for s in range(sections):
        for b in range(4):
            ft[s, b] = feats[s][:, b * 256 : (b + 1) * 256].T
    for j in range(hidden_blocks):
        cols = slice(j * 256, (j + 1) * 256)
        for s in range(sections):
            term = jnp.dot(ft[s, tab[s, j]], grad[:, cols], preferred_element_type=jnp.float32).astype(jnp.bfloat16)
            for x in range(XS):
                terms[x, s * 64 : (s + 1) * 64, cols] = term[x * 64 : (x + 1) * 64]
    for x in range(XS):
        rows = jnp.dot(order[...], terms[x], preferred_element_type=jnp.float32).astype(jnp.bfloat16)
        keep[x] = rows[:128]
        send[x] = rows[128:]


def share_kernel(tab, grad, wn, s0, s1, s2, s3, total):
    shares = (s0, s1, s2, s3)
    sections, hidden_blocks = tab.shape
    for s in range(sections):
        total[...] = jnp.zeros_like(total)
        for j in range(hidden_blocks):
            cols = slice(j * 256, (j + 1) * 256)
            place = columns_of(tab[s, j])
            total[:, place] += lax.dot_general(
                grad[:, cols], wn[s, :, cols], (((1,), (1,)), ((), ())), preferred_element_type=jnp.float32
            )
        shares[s][...] = total[...].astype(jnp.bfloat16)


def orders():
    core, half = lax.axis_index("core"), lax.axis_index("zh")
    row = lax.broadcasted_iota(jnp.int32, (256, 256), 0)
    col = lax.broadcasted_iota(jnp.int32, (256, 256), 1)

    def natural(s, z, y, c, r):
        return s * 64 + z * 32 + y * 8 + c * 4 + r

    stored = natural(
        (col // 4) % 4, ((col // 64) % 2) ^ half, (col // 16) % 4, (col // 128) ^ core, col % 4
    )
    gather = (row == stored).astype(jnp.bfloat16)
    sent = natural((row // 4) % 4, (row // 16) % 2, (row // 32) % 4, (row // 128) ^ core, row % 4)
    scatter = (col == sent).astype(jnp.bfloat16)
    return gather, scatter


def spread(shard):
    everyone = jnp.broadcast_to(shard[None], (XS * YS, *shard.shape))
    got = lax.all_to_all(everyone, PLANE, split_axis=0, concat_axis=0, tiled=True)
    return got.reshape(XS, YS * shard.shape[0], shard.shape[1])


def body(features, weight, block_table, upstream):
    tok_rows = features.shape[0]
    sections, shard_rows, width = weight.shape
    bf16 = jnp.bfloat16
    gather, scatter = orders()

    shard = weight.reshape(sections * shard_rows, width)
    w00 = spread(shard)
    far = flipped(shard, "zh")
    feats = [features]
    for bit in range(3):
        feats.append(swapped(features, bit))
    w10 = flipped(w00, "core")
    w01 = spread(far)
    w11 = flipped(w01, "core")

    act, grad, wn = pl.pallas_call(
        forward_kernel,
        out_shape=(
            jax.ShapeDtypeStruct((tok_rows, width), bf16),
            jax.ShapeDtypeStruct((tok_rows, width), bf16),
            jax.ShapeDtypeStruct((sections, 256, width), bf16),
        ),
        in_specs=[smem()] + [vmem()] * 10,
        out_specs=(vmem(), vmem(), vmem()),
        compiler_params=params(),
        name="forward",
    )(block_table, *feats, w00, w01, w10, w11, upstream, gather)

    half_shape = jax.ShapeDtypeStruct((XS, 128, width), bf16)
    keep, send = pl.pallas_call(
        weight_kernel,
        out_shape=(half_shape, half_shape),
        in_specs=[smem()] + [vmem()] * 6,
        out_specs=(vmem(), vmem()),
        scratch_shapes=[
            pltpu.VMEM((sections, 4, 256, tok_rows), bf16),
            pltpu.VMEM((XS, 256, width), bf16),
        ],
        compiler_params=params(),
        name="weight_grad",
    )(block_table, *feats, grad, scatter)
    got = flipped(send, "core")

    share = jax.ShapeDtypeStruct((tok_rows, features.shape[1]), bf16)
    shares = pl.pallas_call(
        share_kernel,
        out_shape=(share,) * 4,
        in_specs=[smem()] + [vmem()] * 2,
        out_specs=(vmem(),) * 4,
        scratch_shapes=[pltpu.VMEM((tok_rows, features.shape[1]), jnp.float32)],
        compiler_params=params(),
        name="shares",
    )(block_table, grad, wn)

    both = (keep.astype(jnp.float32) + got.astype(jnp.float32)).astype(bf16)
    both = both.reshape(XS * YS, 32, width)
    spread_rows = lax.all_to_all(both, PLANE, split_axis=0, concat_axis=0, tiled=True)
    arrived = []
    for bit in range(3):
        arrived.append(swapped(shares[bit + 1], bit))
    summed = jnp.sum(spread_rows.astype(jnp.float32), axis=0)
    half = lax.axis_index("zh")
    mine = lax.dynamic_slice_in_dim(summed, half * 16, 16, 0)
    other = lax.dynamic_slice_in_dim(summed, (1 - half) * 16, 16, 0).astype(bf16)
    other = flipped(other, "zh")
    scale = float(tok_rows * XS * ZS * YS * CS) ** -0.5
    weight_grad = ((mine + other.astype(jnp.float32)) * scale).reshape(sections, shard_rows, width)

    input_grad = shares[0].astype(jnp.float32)
    for part in arrived:
        input_grad = input_grad + part.astype(jnp.float32)
    return act, input_grad.astype(bf16), weight_grad


def solution(mesh):
    fine = Mesh(mesh.devices.reshape(XS, ZS, YS, CS, mesh.shape["bfly"]), (*DP, "bfly"))
    return jax.shard_map(
        body,
        mesh=fine,
        in_specs=(P(DP, "bfly"), P(None, DP, "bfly"), P(None, "bfly"), P(DP, "bfly")),
        out_specs=(P(DP, "bfly"), P(DP, "bfly"), P(None, DP, "bfly")),
        check_vma=False,
    )
```

```python
import jax
import jax.numpy as jnp
from jax import lax
from jax.experimental import pallas as pl
from jax.experimental.pallas import tpu as pltpu
from jax.sharding import Mesh
from jax.sharding import PartitionSpec as P


half_root = 0.7071067811865476
inv_root_tau = 0.3989422804014327
XS, ZS, YS, CS = 4, 2, 4, 2
DP = ("x", "zh", "y", "core")
PLANE = ("x", "y")
VMEM_LIMIT = 14 * 1024 * 1024


def swapped(block, stride):
    count = lax.axis_size("bfly")
    return lax.ppermute(block, "bfly", [(low, low ^ (1 << stride)) for low in range(count)])


def flipped(block, axis):
    return lax.ppermute(block, axis, [(0, 1), (1, 0)])


def vmem():
    return pl.BlockSpec(memory_space=pltpu.VMEM)


def smem():
    return pl.BlockSpec(memory_space=pltpu.SMEM)


def params(limit=VMEM_LIMIT):
    return pltpu.CompilerParams(vmem_limit_bytes=limit)


def columns_of(block):
    return pl.ds(pl.multiple_of(block * 256, 256), 256)


def grid_of(rows):
    return tuple(lax.broadcasted_iota(jnp.int32, (rows, 256), axis) for axis in (0, 1))


def natural(section, z, y, core, row):
    return section * 64 + z * 32 + y * 8 + core * 4 + row


def gather_order():
    core, half = lax.axis_index("core"), lax.axis_index("zh")
    row, col = grid_of(256)
    stored = natural((col >> 2) & 3, ((col >> 6) & 1) ^ half, (col >> 4) & 3, (col >> 7) ^ core, col & 3)
    return (row == stored).astype(jnp.bfloat16)


def scatter_order():
    row, col = grid_of(128)
    sent = natural((row >> 2) & 3, row >> 6, (row >> 4) & 3, lax.axis_index("core"), row & 3)
    return (col == sent).astype(jnp.bfloat16)


def forward_kernel(tab, f0, f1, f2, f3, w00, w01, w10, w11, up_hbm, act, pack, wn, up, sem):
    feats = (f0, f1, f2, f3)
    sections, hidden_blocks = tab.shape
    fetch = pltpu.make_async_copy(up_hbm, up, sem)
    fetch.start()
    order = gather_order()
    for x in range(XS):
        rows = jnp.concatenate([w00[x], w01[x], w10[x], w11[x]], axis=0)
        ordered = jnp.dot(order, rows, preferred_element_type=jnp.float32).astype(jnp.bfloat16)
        for s in range(sections):
            wn[s, x * 64 : (x + 1) * 64, :] = ordered[s * 64 : (s + 1) * 64]
    edge = f3.shape[1]
    pack[:, :edge] = f3[...]
    fetch.wait()
    for j in range(hidden_blocks):
        cols = slice(j * 256, (j + 1) * 256)
        spot = slice(edge + j * 256, edge + (j + 1) * 256)
        pre = None
        for s in range(sections):
            term = jnp.dot(feats[s][:, columns_of(tab[s, j])], wn[s, :, cols], preferred_element_type=jnp.float32)
            pre = term if pre is None else pre + term
        cdf = 0.5 * (1.0 + lax.erf(pre * half_root))
        density = jnp.exp(-0.5 * pre * pre) * inv_root_tau
        act[:, cols] = (pre * cdf).astype(jnp.bfloat16)
        pack[:, spot] = (up[:, cols].astype(jnp.float32) * (cdf + pre * density)).astype(jnp.bfloat16)


def halved(into, rows):
    for x in range(XS):
        for z in range(ZS):
            start = x * 64 + z * 32
            into[z, x * 32 : (x + 1) * 32] = rows[start : start + 32]


def turn_kernel(f0, f1, f2, ft):
    for s, feats in enumerate((f0, f1, f2)):
        for b in range(4):
            halved(ft.at[s, b], feats[:, b * 256 : (b + 1) * 256].T)


def weight_rows(z, tab, ft0, ft1, last, pack0, pack1, out, terms):
    sections, hidden_blocks = tab.shape
    edge = last.shape[0] * 256
    for j in range(hidden_blocks):
        cols = slice(j * 256, (j + 1) * 256)
        spot = slice(edge + j * 256, edge + (j + 1) * 256)
        grad = jnp.concatenate([pack0[:, spot], pack1[:, spot]], axis=0)
        for s in range(sections):
            b = tab[s, j]
            turned = jnp.concatenate([ft0[s, b, z], ft1[s, b, z]], axis=1) if s < sections - 1 else last[b, z]
            term = jnp.dot(turned, grad, preferred_element_type=jnp.float32).astype(jnp.bfloat16)
            for pair in range(2):
                terms[pair, s * 64 : (s + 1) * 64, cols] = term[pair * 64 : (pair + 1) * 64]
    order = scatter_order()
    for pair in range(2):
        out[pair] = jnp.dot(order, terms[pair], preferred_element_type=jnp.float32).astype(jnp.bfloat16)


def far_kernel(tab, ft0, ft1, pack0, pack1, out, last, terms):
    for b in range(4):
        cols = slice(b * 256, (b + 1) * 256)
        halved(last.at[b], jnp.concatenate([pack0[:, cols].T, pack1[:, cols].T], axis=1))
    weight_rows(1 - lax.axis_index("zh"), tab, ft0, ft1, last, pack0, pack1, out, terms)


def near_kernel(tab, ft0, ft1, last, pack0, pack1, out, terms):
    weight_rows(lax.axis_index("zh"), tab, ft0, ft1, last, pack0, pack1, out, terms)


def share_kernel(tab, pack, wn, s0, s1, s2, s3, total):
    shares = (s0, s1, s2, s3)
    edge = s0.shape[1]
    sections, hidden_blocks = tab.shape
    for s in range(sections):
        total[...] = jnp.zeros_like(total)
        for j in range(hidden_blocks):
            cols = slice(j * 256, (j + 1) * 256)
            spot = slice(edge + j * 256, edge + (j + 1) * 256)
            place = columns_of(tab[s, j])
            total[:, place] += lax.dot_general(
                pack[:, spot], wn[s, :, cols], (((1,), (1,)), ((), ())), preferred_element_type=jnp.float32
            )
        shares[s][...] = total[...].astype(jnp.bfloat16)


def repeat_kernel(shard, out):
    for peer in range(out.shape[0]):
        out[peer] = shard[...]


def exchanged(rows):
    return lax.all_to_all(rows, PLANE, split_axis=0, concat_axis=0, tiled=True)


def spread(shard):
    everyone = pl.pallas_call(
        repeat_kernel,
        out_shape=jax.ShapeDtypeStruct((XS * YS, *shard.shape), shard.dtype),
        in_specs=[vmem()],
        out_specs=vmem(),
        compiler_params=params(4 * 1024 * 1024),
        name="repeat",
    )(shard)
    got = exchanged(everyone)
    return got.reshape(XS, YS * shard.shape[0], shard.shape[1])


def body(features, weight, block_table, upstream):
    tok_rows = features.shape[0]
    sections, shard_rows, width = weight.shape
    bf16 = jnp.bfloat16
    shard = weight.reshape(sections * shard_rows, width)
    w00 = spread(shard)
    far = flipped(shard, "zh")
    feats = [features]
    for bit in range(3):
        feats.append(swapped(features, bit))
    w10 = flipped(w00, "core")
    w01 = spread(far)
    w11 = flipped(w01, "core")

    turned = pl.pallas_call(
        turn_kernel,
        out_shape=jax.ShapeDtypeStruct((sections - 1, 4, ZS, 128, tok_rows), bf16),
        in_specs=[vmem()] * 3,
        out_specs=vmem(),
        compiler_params=params(),
        name="turn",
    )(*feats[:3])
    turned_got = flipped(turned, "core")

    edge = features.shape[1]
    act, pack, wn = pl.pallas_call(
        forward_kernel,
        out_shape=(
            jax.ShapeDtypeStruct((tok_rows, width), bf16),
            jax.ShapeDtypeStruct((tok_rows, edge + width), bf16),
            jax.ShapeDtypeStruct((sections, 256, width), bf16),
        ),
        in_specs=[smem()] + [vmem()] * 8 + [pl.BlockSpec(memory_space=pltpu.MemorySpace.HBM)],
        out_specs=(vmem(), vmem(), vmem()),
        scratch_shapes=[pltpu.VMEM((tok_rows, width), bf16), pltpu.SemaphoreType.DMA],
        compiler_params=params(),
        name="forward",
    )(block_table, *feats, w00, w01, w10, w11, upstream)
    pack_got = flipped(pack, "core")

    share = jax.ShapeDtypeStruct((tok_rows, edge), bf16)
    shares = pl.pallas_call(
        share_kernel,
        out_shape=(share,) * 4,
        in_specs=[smem()] + [vmem()] * 2,
        out_specs=(vmem(),) * 4,
        scratch_shapes=[pltpu.VMEM((tok_rows, edge), jnp.float32)],
        compiler_params=params(),
        name="shares",
    )(block_table, pack, wn)

    rows_shape = jax.ShapeDtypeStruct((2, 128, width), bf16)
    last_shape = jax.ShapeDtypeStruct((4, ZS, 128, 2 * tok_rows), bf16)
    terms = [pltpu.VMEM((2, 256, width), bf16)]
    far_rows, last = pl.pallas_call(
        far_kernel,
        out_shape=(rows_shape, last_shape),
        in_specs=[smem()] + [vmem()] * 4,
        out_specs=(vmem(), vmem()),
        scratch_shapes=terms,
        compiler_params=params(),
        name="far_rows",
    )(block_table, turned, turned_got, pack, pack_got)
    far_got = exchanged(far_rows.reshape(XS * YS, 16, width))
    near_rows = pl.pallas_call(
        near_kernel,
        out_shape=rows_shape,
        in_specs=[smem()] + [vmem()] * 5,
        out_specs=vmem(),
        scratch_shapes=terms,
        compiler_params=params(),
        name="near_rows",
    )(block_table, turned, turned_got, last, pack, pack_got)
    arrived = []
    for bit in range(3):
        arrived.append(swapped(shares[bit + 1], bit))
    near_got = exchanged(near_rows.reshape(XS * YS, 16, width))
    far_sum = jnp.sum(far_got.astype(jnp.float32), axis=0).astype(bf16)
    other = flipped(far_sum, "zh")
    mine = jnp.sum(near_got.astype(jnp.float32), axis=0)
    scale = float(tok_rows * XS * ZS * YS * CS) ** -0.5
    weight_grad = ((mine + other.astype(jnp.float32)) * scale).reshape(sections, shard_rows, width)

    input_grad = shares[0].astype(jnp.float32)
    for part in arrived:
        input_grad = input_grad + part.astype(jnp.float32)
    input_grad = input_grad.astype(bf16)
    return act, input_grad, weight_grad


def solution(mesh):
    fine = Mesh(mesh.devices.reshape(XS, ZS, YS, CS, mesh.shape["bfly"]), (*DP, "bfly"))
    return jax.shard_map(
        body,
        mesh=fine,
        in_specs=(P(DP, "bfly"), P(None, DP, "bfly"), P(None, "bfly"), P(DP, "bfly")),
        out_specs=(P(DP, "bfly"), P(DP, "bfly"), P(None, DP, "bfly")),
        check_vma=False,
    )
```

```python
import jax
import jax.numpy as jnp
from jax import lax
from jax.experimental import pallas as pl
from jax.experimental.pallas import tpu as pltpu
from jax.sharding import Mesh
from jax.sharding import PartitionSpec as P


half_root = 0.7071067811865476
inv_root_tau = 0.3989422804014327
XS, ZS, YS, CS = 4, 2, 4, 2
DP = ("x", "zh", "y", "core")
PLANE = ("x", "y")
VMEM_LIMIT = 14 * 1024 * 1024


def swapped(block, stride):
    count = lax.axis_size("bfly")
    return lax.ppermute(block, "bfly", [(low, low ^ (1 << stride)) for low in range(count)])


def flipped(block, axis):
    return lax.ppermute(block, axis, [(0, 1), (1, 0)])


def vmem():
    return pl.BlockSpec(memory_space=pltpu.VMEM)


def hbm():
    return pl.BlockSpec(memory_space=pltpu.MemorySpace.HBM)


def in_hbm(array):
    return pltpu.with_memory_space_constraint(array, pltpu.MemorySpace.HBM)


def smem():
    return pl.BlockSpec(memory_space=pltpu.SMEM)


def params(limit=VMEM_LIMIT):
    return pltpu.CompilerParams(vmem_limit_bytes=limit)


def columns_of(block):
    return pl.ds(pl.multiple_of(block * 256, 256), 256)


def grid_of(rows):
    return tuple(lax.broadcasted_iota(jnp.int32, (rows, 256), axis) for axis in (0, 1))


def natural(section, z, y, core, row):
    return section * 64 + z * 32 + y * 8 + core * 4 + row


def gather_order():
    core, half = lax.axis_index("core"), lax.axis_index("zh")
    row, col = grid_of(256)
    stored = natural((col >> 2) & 3, ((col >> 6) & 1) ^ half, (col >> 4) & 3, (col >> 7) ^ core, col & 3)
    return (row == stored).astype(jnp.bfloat16)


def scatter_order():
    row, col = grid_of(128)
    sent = natural((row >> 2) & 3, row >> 6, (row >> 4) & 3, lax.axis_index("core"), row & 3)
    return (col == sent).astype(jnp.bfloat16)


def forward_kernel(tab, g0, g1, g2, g3, w00, w01, w10, w11, up_hbm, act, pack, wn, f0, f1, f2, f3, up, sems):
    feats = (f0, f1, f2, f3)
    sections, hidden_blocks = tab.shape
    moves = zip((g0, g1, g2, g3, up_hbm), (f0, f1, f2, f3, up), range(5))
    fetches = [pltpu.make_async_copy(source, target, sems.at[i]) for source, target, i in moves]
    for fetch in fetches:
        fetch.start()
    order = gather_order()
    for x in range(XS):
        rows = jnp.concatenate([w00[x], w01[x], w10[x], w11[x]], axis=0)
        ordered = jnp.dot(order, rows, preferred_element_type=jnp.float32).astype(jnp.bfloat16)
        for s in range(sections):
            wn[s, x * 64 : (x + 1) * 64, :] = ordered[s * 64 : (s + 1) * 64]
    for fetch in fetches:
        fetch.wait()
    edge = f3.shape[1]
    pack[:, :edge] = f3[...]
    for j in range(hidden_blocks):
        cols = slice(j * 256, (j + 1) * 256)
        spot = slice(edge + j * 256, edge + (j + 1) * 256)
        pre = None
        for s in range(sections):
            term = jnp.dot(feats[s][:, columns_of(tab[s, j])], wn[s, :, cols], preferred_element_type=jnp.float32)
            pre = term if pre is None else pre + term
        cdf = 0.5 * (1.0 + lax.erf(pre * half_root))
        density = jnp.exp(-0.5 * pre * pre) * inv_root_tau
        act[:, cols] = (pre * cdf).astype(jnp.bfloat16)
        pack[:, spot] = (up[:, cols].astype(jnp.float32) * (cdf + pre * density)).astype(jnp.bfloat16)


def halved(into, rows):
    for x in range(XS):
        for z in range(ZS):
            start = x * 64 + z * 32
            into[z, x * 32 : (x + 1) * 32] = rows[start : start + 32]


def turn_kernel(f0, f1, f2, ft):
    for s, feats in enumerate((f0, f1, f2)):
        for b in range(4):
            halved(ft.at[s, b], feats[:, b * 256 : (b + 1) * 256].T)


def weight_rows(z, tab, ft0, ft1, last, pack0, pack1, out, terms):
    sections, hidden_blocks = tab.shape
    edge = last.shape[0] * 256
    for j in range(hidden_blocks):
        cols = slice(j * 256, (j + 1) * 256)
        spot = slice(edge + j * 256, edge + (j + 1) * 256)
        grad = jnp.concatenate([pack0[:, spot], pack1[:, spot]], axis=0)
        for s in range(sections):
            b = tab[s, j]
            turned = jnp.concatenate([ft0[s, b, z], ft1[s, b, z]], axis=1) if s < sections - 1 else last[b, z]
            term = jnp.dot(turned, grad, preferred_element_type=jnp.float32).astype(jnp.bfloat16)
            for pair in range(2):
                terms[pair, s * 64 : (s + 1) * 64, cols] = term[pair * 64 : (pair + 1) * 64]
    order = scatter_order()
    for pair in range(2):
        out[pair] = jnp.dot(order, terms[pair], preferred_element_type=jnp.float32).astype(jnp.bfloat16)


def far_kernel(tab, ft0, ft1, pack0, pack1, out, last, terms):
    for b in range(4):
        cols = slice(b * 256, (b + 1) * 256)
        halved(last.at[b], jnp.concatenate([pack0[:, cols].T, pack1[:, cols].T], axis=1))
    weight_rows(1 - lax.axis_index("zh"), tab, ft0, ft1, last, pack0, pack1, out, terms)


def near_kernel(tab, ft0, ft1, last, pack0, pack1, out, terms):
    weight_rows(lax.axis_index("zh"), tab, ft0, ft1, last, pack0, pack1, out, terms)


def share_kernel(tab, pack, wn, s0, s1, s2, s3, total):
    shares = (s0, s1, s2, s3)
    edge = s0.shape[1]
    sections, hidden_blocks = tab.shape
    for s in range(sections):
        total[...] = jnp.zeros_like(total)
        for j in range(hidden_blocks):
            cols = slice(j * 256, (j + 1) * 256)
            spot = slice(edge + j * 256, edge + (j + 1) * 256)
            place = columns_of(tab[s, j])
            total[:, place] += lax.dot_general(
                pack[:, spot], wn[s, :, cols], (((1,), (1,)), ((), ())), preferred_element_type=jnp.float32
            )
        shares[s][...] = total[...].astype(jnp.bfloat16)


def repeat_kernel(shard, out):
    for peer in range(out.shape[0]):
        out[peer] = shard[...]


def exchanged(rows):
    return lax.all_to_all(rows, PLANE, split_axis=0, concat_axis=0, tiled=True)


def spread(shard):
    everyone = pl.pallas_call(
        repeat_kernel,
        out_shape=jax.ShapeDtypeStruct((XS * YS, *shard.shape), shard.dtype),
        in_specs=[vmem()],
        out_specs=vmem(),
        compiler_params=params(4 * 1024 * 1024),
        name="repeat",
    )(shard)
    got = exchanged(everyone)
    return got.reshape(XS, YS * shard.shape[0], shard.shape[1])


def body(features, weight, block_table, upstream):
    tok_rows = features.shape[0]
    sections, shard_rows, width = weight.shape
    bf16 = jnp.bfloat16
    shard = weight.reshape(sections * shard_rows, width)
    w00 = spread(shard)
    far = flipped(shard, "zh")
    feats = [features]
    for bit in range(3):
        feats.append(swapped(features, bit))
    w10 = flipped(w00, "core")
    w01 = spread(far)
    w11 = flipped(w01, "core")

    turned = pl.pallas_call(
        turn_kernel,
        out_shape=jax.ShapeDtypeStruct((sections - 1, 4, ZS, 128, tok_rows), bf16),
        in_specs=[vmem()] * 3,
        out_specs=vmem(),
        compiler_params=params(),
        name="turn",
    )(*feats[:3])
    turned_got = flipped(turned, "core")

    edge = features.shape[1]
    act, pack, wn = pl.pallas_call(
        forward_kernel,
        out_shape=(
            jax.ShapeDtypeStruct((tok_rows, width), bf16),
            jax.ShapeDtypeStruct((tok_rows, edge + width), bf16),
            jax.ShapeDtypeStruct((sections, 256, width), bf16),
        ),
        in_specs=[smem()] + [hbm()] * 4 + [vmem()] * 4 + [hbm()],
        out_specs=(vmem(), vmem(), vmem()),
        scratch_shapes=[pltpu.VMEM((tok_rows, edge), bf16)] * 4
        + [pltpu.VMEM((tok_rows, width), bf16), pltpu.SemaphoreType.DMA((5,))],
        compiler_params=params(),
        name="forward",
    )(block_table, *map(in_hbm, feats), w00, w01, w10, w11, in_hbm(upstream))
    pack_got = flipped(pack, "core")

    share = jax.ShapeDtypeStruct((tok_rows, edge), bf16)
    shares = pl.pallas_call(
        share_kernel,
        out_shape=(share,) * 4,
        in_specs=[smem()] + [vmem()] * 2,
        out_specs=(vmem(),) * 4,
        scratch_shapes=[pltpu.VMEM((tok_rows, edge), jnp.float32)],
        compiler_params=params(),
        name="shares",
    )(block_table, pack, wn)

    rows_shape = jax.ShapeDtypeStruct((2, 128, width), bf16)
    last_shape = jax.ShapeDtypeStruct((4, ZS, 128, 2 * tok_rows), bf16)
    terms = [pltpu.VMEM((2, 256, width), bf16)]
    far_rows, last = pl.pallas_call(
        far_kernel,
        out_shape=(rows_shape, last_shape),
        in_specs=[smem()] + [vmem()] * 4,
        out_specs=(vmem(), vmem()),
        scratch_shapes=terms,
        compiler_params=params(),
        name="far_rows",
    )(block_table, turned, turned_got, pack, pack_got)
    far_got = exchanged(far_rows.reshape(XS * YS, 16, width))
    near_rows = pl.pallas_call(
        near_kernel,
        out_shape=rows_shape,
        in_specs=[smem()] + [vmem()] * 5,
        out_specs=vmem(),
        scratch_shapes=terms,
        compiler_params=params(),
        name="near_rows",
    )(block_table, turned, turned_got, last, pack, pack_got)
    arrived = []
    for bit in range(3):
        arrived.append(swapped(shares[bit + 1], bit))
    near_got = exchanged(near_rows.reshape(XS * YS, 16, width))
    far_sum = jnp.sum(far_got.astype(jnp.float32), axis=0).astype(bf16)
    other = flipped(far_sum, "zh")
    mine = jnp.sum(near_got.astype(jnp.float32), axis=0)
    scale = float(tok_rows * XS * ZS * YS * CS) ** -0.5
    weight_grad = ((mine + other.astype(jnp.float32)) * scale).reshape(sections, shard_rows, width)

    input_grad = shares[0].astype(jnp.float32)
    for part in arrived:
        input_grad = input_grad + part.astype(jnp.float32)
    input_grad = input_grad.astype(bf16)
    return act, input_grad, weight_grad


def solution(mesh):
    fine = Mesh(mesh.devices.reshape(XS, ZS, YS, CS, mesh.shape["bfly"]), (*DP, "bfly"))
    return jax.shard_map(
        body,
        mesh=fine,
        in_specs=(P(DP, "bfly"), P(None, DP, "bfly"), P(None, "bfly"), P(DP, "bfly")),
        out_specs=(P(DP, "bfly"), P(DP, "bfly"), P(None, DP, "bfly")),
        check_vma=False,
    )
```

```python
import jax
import jax.numpy as jnp
from jax import lax
from jax.experimental import pallas as pl
from jax.experimental.pallas import tpu as pltpu
from jax.sharding import Mesh
from jax.sharding import PartitionSpec as P


half_root = 0.7071067811865476
inv_root_tau = 0.3989422804014327
XS, ZS, YS, CS = 4, 2, 4, 2
DP = ("x", "zh", "y", "core")
PLANE = ("x", "y")
VMEM_LIMIT = 14 * 1024 * 1024


def swapped(block, stride):
    count = lax.axis_size("bfly")
    return lax.ppermute(block, "bfly", [(low, low ^ (1 << stride)) for low in range(count)])


def flipped(block, axis):
    return lax.ppermute(block, axis, [(0, 1), (1, 0)])


def vmem():
    return pl.BlockSpec(memory_space=pltpu.VMEM)


def smem():
    return pl.BlockSpec(memory_space=pltpu.SMEM)


def params(limit=VMEM_LIMIT):
    return pltpu.CompilerParams(vmem_limit_bytes=limit)


def columns_of(block):
    return pl.ds(pl.multiple_of(block * 256, 256), 256)


def grid_of(rows):
    return tuple(lax.broadcasted_iota(jnp.int32, (rows, 256), axis) for axis in (0, 1))


def natural(section, z, y, core, row):
    return section * 64 + z * 32 + y * 8 + core * 4 + row


def gather_order():
    core, half = lax.axis_index("core"), lax.axis_index("zh")
    row, col = grid_of(256)
    stored = natural((col >> 2) & 3, ((col >> 6) & 1) ^ half, (col >> 4) & 3, (col >> 7) ^ core, col & 3)
    return (row == stored).astype(jnp.bfloat16)


def scatter_order():
    row, col = grid_of(128)
    sent = natural((row >> 2) & 3, (row >> 4) & 1, row >> 5, lax.axis_index("core"), row & 3)
    return (col == sent).astype(jnp.bfloat16)


def forward_kernel(tab, f0, f1, f2, f3, w00, w01, w10, w11, up_hbm, act, pack, wn, up, sem):
    feats = (f0, f1, f2, f3)
    sections, hidden_blocks = tab.shape
    fetch = pltpu.make_async_copy(up_hbm, up, sem)
    fetch.start()
    order = gather_order()
    for x in range(XS):
        rows = jnp.concatenate([w00[x], w01[x], w10[x], w11[x]], axis=0)
        ordered = jnp.dot(order, rows, preferred_element_type=jnp.float32).astype(jnp.bfloat16)
        for s in range(sections):
            wn[s, x * 64 : (x + 1) * 64, :] = ordered[s * 64 : (s + 1) * 64]
    edge = f3.shape[1]
    pack[:, :edge] = f3[...]
    fetch.wait()
    for j in range(hidden_blocks):
        cols = slice(j * 256, (j + 1) * 256)
        spot = slice(edge + j * 256, edge + (j + 1) * 256)
        pre = None
        for s in range(sections):
            term = jnp.dot(feats[s][:, columns_of(tab[s, j])], wn[s, :, cols], preferred_element_type=jnp.float32)
            pre = term if pre is None else pre + term
        cdf = 0.5 * (1.0 + lax.erf(pre * half_root))
        density = jnp.exp(-0.5 * pre * pre) * inv_root_tau
        act[:, cols] = (pre * cdf).astype(jnp.bfloat16)
        pack[:, spot] = (up[:, cols].astype(jnp.float32) * (cdf + pre * density)).astype(jnp.bfloat16)


def turn_kernel(f0, f1, f2, ft):
    for s, feats in enumerate((f0, f1, f2)):
        for b in range(4):
            ft[s, b] = feats[:, b * 256 : (b + 1) * 256].T


def weight_kernel(tab, ft0, ft1, pack0, pack1, out, last, terms):
    sections, hidden_blocks = tab.shape
    edge = last.shape[0] * 256
    for b in range(4):
        cols = slice(b * 256, (b + 1) * 256)
        last[b] = jnp.concatenate([pack0[:, cols].T, pack1[:, cols].T], axis=1)
    for j in range(hidden_blocks):
        cols = slice(j * 256, (j + 1) * 256)
        spot = slice(edge + j * 256, edge + (j + 1) * 256)
        grad = jnp.concatenate([pack0[:, spot], pack1[:, spot]], axis=0)
        for s in range(sections):
            b = tab[s, j]
            turned = jnp.concatenate([ft0[s, b], ft1[s, b]], axis=1) if s < sections - 1 else last[b]
            term = jnp.dot(turned, grad, preferred_element_type=jnp.float32).astype(jnp.bfloat16)
            for x in range(XS):
                terms[x, s * 64 : (s + 1) * 64, cols] = term[x * 64 : (x + 1) * 64]
    order = scatter_order()
    for x in range(XS):
        out[x] = jnp.dot(order, terms[x], preferred_element_type=jnp.float32).astype(jnp.bfloat16)


def share_kernel(tab, pack, wn, s0, s1, s2, s3, total):
    shares = (s0, s1, s2, s3)
    edge = s0.shape[1]
    sections, hidden_blocks = tab.shape
    for s in range(sections):
        total[...] = jnp.zeros_like(total)
        for j in range(hidden_blocks):
            cols = slice(j * 256, (j + 1) * 256)
            spot = slice(edge + j * 256, edge + (j + 1) * 256)
            place = columns_of(tab[s, j])
            total[:, place] += lax.dot_general(
                pack[:, spot], wn[s, :, cols], (((1,), (1,)), ((), ())), preferred_element_type=jnp.float32
            )
        shares[s][...] = total[...].astype(jnp.bfloat16)


def spread(shard):
    everyone = jnp.broadcast_to(shard[None], (XS * YS, *shard.shape))
    got = lax.all_to_all(everyone, PLANE, split_axis=0, concat_axis=0, tiled=True)
    return got.reshape(XS, YS * shard.shape[0], shard.shape[1])


def body(features, weight, block_table, upstream):
    tok_rows = features.shape[0]
    sections, shard_rows, width = weight.shape
    bf16 = jnp.bfloat16
    shard = weight.reshape(sections * shard_rows, width)
    w00 = spread(shard)
    far = flipped(shard, "zh")
    feats = [features]
    for bit in range(3):
        feats.append(swapped(features, bit))
    w10 = flipped(w00, "core")
    w01 = spread(far)
    w11 = flipped(w01, "core")

    turned = pl.pallas_call(
        turn_kernel,
        out_shape=jax.ShapeDtypeStruct((sections - 1, 4, 256, tok_rows), bf16),
        in_specs=[vmem()] * 3,
        out_specs=vmem(),
        compiler_params=params(),
        name="turn",
    )(*feats[:3])
    turned_got = flipped(turned, "core")

    edge = features.shape[1]
    act, pack, wn = pl.pallas_call(
        forward_kernel,
        out_shape=(
            jax.ShapeDtypeStruct((tok_rows, width), bf16),
            jax.ShapeDtypeStruct((tok_rows, edge + width), bf16),
            jax.ShapeDtypeStruct((sections, 256, width), bf16),
        ),
        in_specs=[smem()] + [vmem()] * 8 + [pl.BlockSpec(memory_space=pltpu.MemorySpace.HBM)],
        out_specs=(vmem(), vmem(), vmem()),
        scratch_shapes=[pltpu.VMEM((tok_rows, width), bf16), pltpu.SemaphoreType.DMA],
        compiler_params=params(),
        name="forward",
    )(block_table, *feats, w00, w01, w10, w11, pltpu.with_memory_space_constraint(upstream, pltpu.MemorySpace.HBM))
    pack_got = flipped(pack, "core")

    share = jax.ShapeDtypeStruct((tok_rows, edge), bf16)
    shares = pl.pallas_call(
        share_kernel,
        out_shape=(share,) * 4,
        in_specs=[smem()] + [vmem()] * 2,
        out_specs=(vmem(),) * 4,
        scratch_shapes=[pltpu.VMEM((tok_rows, edge), jnp.float32)],
        compiler_params=params(),
        name="shares",
    )(block_table, pack, wn)

    both = pl.pallas_call(
        weight_kernel,
        out_shape=jax.ShapeDtypeStruct((XS, 128, width), bf16),
        in_specs=[smem()] + [vmem()] * 4,
        out_specs=vmem(),
        scratch_shapes=[
            pltpu.VMEM((4, 256, 2 * tok_rows), bf16),
            pltpu.VMEM((XS, 256, width), bf16),
        ],
        compiler_params=params(),
        name="weight_grad",
    )(block_table, turned, turned_got, pack, pack_got)
    both = both.reshape(XS * YS, 32, width)
    spread_rows = lax.all_to_all(both, PLANE, split_axis=0, concat_axis=0, tiled=True)
    arrived = []
    for bit in range(3):
        arrived.append(swapped(shares[bit + 1], bit))
    summed = jnp.sum(spread_rows.astype(jnp.float32), axis=0)
    half = lax.axis_index("zh")
    mine = lax.dynamic_slice_in_dim(summed, half * 16, 16, 0)
    other = lax.dynamic_slice_in_dim(summed, (1 - half) * 16, 16, 0).astype(bf16)
    other = flipped(other, "zh")
    scale = float(tok_rows * XS * ZS * YS * CS) ** -0.5
    weight_grad = ((mine + other.astype(jnp.float32)) * scale).reshape(sections, shard_rows, width)

    input_grad = shares[0].astype(jnp.float32)
    for part in arrived:
        input_grad = input_grad + part.astype(jnp.float32)
    return act, input_grad.astype(bf16), weight_grad


def solution(mesh):
    fine = Mesh(mesh.devices.reshape(XS, ZS, YS, CS, mesh.shape["bfly"]), (*DP, "bfly"))
    return jax.shard_map(
        body,
        mesh=fine,
        in_specs=(P(DP, "bfly"), P(None, DP, "bfly"), P(None, "bfly"), P(DP, "bfly")),
        out_specs=(P(DP, "bfly"), P(DP, "bfly"), P(None, DP, "bfly")),
        check_vma=False,
    )
```
